768 devices in a mesh: dp: 32 (over y, x), seq: 4 (over z_hi), tensor: 6 (over z_lo, core).
Axes of the slice: x: 4, y: 8, z: 12 (z_hi: 4, z_lo: 3; z = z_hi * 3 + z_lo), core: 2. Of those that a mesh axis runs over, the one named last changes fastest.
Arguments:
- memory_in: bfloat16 [192, 588, 1024], P(('dp', 'tensor'), 'seq'), may hold values from -6 to 6
- norm_gain: float32 [1024], replicated, may hold values from 0.1 to 1.9
- qkv_weight: bfloat16 [1024, 1536], replicated, may hold values from -1 to 1
- out_weight: bfloat16 [512, 1024], replicated, may hold values from -0.25 to 0.25
- key_weight: bfloat16 [1024, 1024], replicated, may hold values from -0.1875 to 0.1875
- value_weight: bfloat16 [1024, 1024], replicated, may hold values from -0.1875 to 0.1875
- shift_offsets: int32 [192, 2], P(('dp', 'tensor')), may hold values from 1 to 6
- row_order: int32 [192, 588], P('dp'), may hold values from 0 to 587, each once within a row
Outputs:
- keys: bfloat16 [192, 588, 1024], P('dp', 'tensor', 'seq')
- values: bfloat16 [192, 588, 1024], P('dp', 'tensor', 'seq')
The draws below stay inside these ranges and needn't reach their ends.
All inputs are finite; a program needn't handle non-finite values.
Results may differ from the reference program's by a relative error of at most 0.008.
Values may be sent and summed in bfloat16 or wider, within the bound.
A program may use at most 64 MiB of HBM per device.

```python
import jax
import jax.numpy as jnp
from jax import lax

EMB = 1024
HEADS = 16
HEAD_DIM = 32
GRID_H = 28
GRID_W = 21
WIN = 7
ROWS = 588
KVW = 1024
PAGES = 192


def draw_memory_in(key, part):
    sample = jnp.clip(jax.random.normal(jax.random.fold_in(key, 23), (PAGES, ROWS, EMB), jnp.float32), -6.0, 6.0)
    return sample.astype(jnp.bfloat16)


def draw_qkv_weight(key, part):
    attn_width = HEADS * HEAD_DIM
    total_width = 3 * attn_width
    sample = jnp.clip(jax.random.normal(jax.random.fold_in(key, 34), (EMB, total_width), jnp.float32), -6.0, 6.0) * EMB ** (-0.5)
    return sample.astype(jnp.bfloat16)


def set_ends(drawn, key, smallest, high):
    shape = drawn.shape
    spot = [jax.random.randint(jax.random.fold_in(key, axis), (), 0, shape[axis]) for axis in range(len(shape))]
    drawn = drawn.at[tuple(spot)].set(smallest)
    longest = shape.index(max(shape))
    spot[longest] = (spot[longest] + 1) % shape[longest]
    return drawn.at[tuple(spot)].set(high)


def scatter_about(key, dims, width, most, held_as=jnp.bfloat16):
    entries = width * jax.random.normal(key, dims, jnp.float32)
    return jnp.clip(entries, min=-most, max=most).astype(held_as)


def setup_inputs(seed: int = 0) -> dict:
    splits = jax.random.split(jax.random.key(seed), 9)
    memory_in = draw_memory_in(jax.random.fold_in(splits[8], 71), 0)
    norm_gain = jnp.clip(1.0 + 0.18 * jax.random.normal(splits[1], (EMB,), jnp.float32), 0.1, 1.9)
    qkv_weight = draw_qkv_weight(jax.random.fold_in(splits[8], 71), 0)
    out_weight = scatter_about(splits[3], (HEADS * HEAD_DIM, EMB), (HEADS * HEAD_DIM) ** -0.5, 0.25)
    key_weight = scatter_about(splits[4], (EMB, KVW), EMB ** -0.5, 0.1875)
    value_weight = scatter_about(splits[5], (EMB, KVW), EMB ** -0.5, 0.1875)
    shift_offsets = set_ends(jax.random.randint(splits[6], (PAGES, 2), 1, WIN), jax.random.fold_in(splits[6], 1), 1, WIN - 1).astype(jnp.int32)
    row_order = jax.vmap(lambda own: jax.random.permutation(own, ROWS))(jax.random.split(splits[7], PAGES)).reshape((PAGES, ROWS)).astype(jnp.int32)
    return dict(memory_in=memory_in, norm_gain=norm_gain, qkv_weight=qkv_weight, out_weight=out_weight, key_weight=key_weight, value_weight=value_weight, shift_offsets=shift_offsets, row_order=row_order)


def window_block(rolled, first_row, row_shift, col_shift, norm_gain, qkv_weight, out_weight):
    row_count = rolled.shape[0] // GRID_W
    attn_width = HEADS * HEAD_DIM
    win_rows = row_count // WIN
    win_cols = GRID_W // WIN
    x_float = rolled.astype(jnp.float32)
    row_mean = lax.optimization_barrier(jnp.mean(x_float, axis=-1, keepdims=True))
    row_var = lax.optimization_barrier(jnp.mean((x_float - row_mean) ** 2, axis=-1, keepdims=True))
    normed = ((x_float - row_mean) * lax.rsqrt(row_var + 1e-05) * norm_gain).astype(jnp.bfloat16)
    projected_qkv = jnp.dot(normed, qkv_weight, preferred_element_type=jnp.float32).astype(jnp.bfloat16)

    def windows(block):
        block = block.reshape(win_rows, WIN, win_cols, WIN, HEADS, HEAD_DIM)
        return block.transpose(0, 2, 4, 1, 3, 5).reshape(win_rows * win_cols, HEADS, WIN * WIN, HEAD_DIM)
    queries = windows(projected_qkv[:, :attn_width]).astype(jnp.float32)
    keys_win = windows(projected_qkv[:, attn_width:2 * attn_width]).astype(jnp.float32)
    values_win = windows(projected_qkv[:, 2 * attn_width:]).astype(jnp.float32)
    scores = jnp.einsum('whqd,whkd->whqk', queries, keys_win) * HEAD_DIM ** (-0.5)
    row_ids = first_row + jnp.arange(row_count, dtype=jnp.int32)
    col_ids = jnp.arange(GRID_W, dtype=jnp.int32)
    wrap_row = (row_ids >= GRID_H - row_shift).astype(jnp.int32)
    wrap_col = (col_ids >= GRID_W - col_shift).astype(jnp.int32)
    labels = 2 * wrap_row[:, None] + wrap_col[None, :]
    labels = labels.reshape(win_rows, WIN, win_cols, WIN).transpose(0, 2, 1, 3).reshape(win_rows * win_cols, WIN * WIN)
    same_region = labels[:, :, None] == labels[:, None, :]
    scores = jnp.where(same_region[:, None], scores, -1000000000.0)
    weights = jax.nn.softmax(scores, axis=-1).astype(jnp.bfloat16)
    attended = jnp.einsum('whqk,whkd->whqd', weights.astype(jnp.float32), values_win).astype(jnp.bfloat16)
    restored = attended.reshape(win_rows, win_cols, HEADS, WIN, WIN, HEAD_DIM)
    restored = restored.transpose(0, 3, 1, 4, 2, 5).reshape(row_count * GRID_W, attn_width)
    return (x_float + jnp.dot(restored, out_weight, preferred_element_type=jnp.float32)).astype(jnp.bfloat16)

def reference(memory_in, norm_gain, qkv_weight, out_weight, key_weight, value_weight, shift_offsets, row_order):

    def per_page(inputs_page):
        page_rows, shifts, row_perm = inputs_page
        page_grid = page_rows.reshape(GRID_H, GRID_W, EMB)
        page_grid = jnp.roll(page_grid, -shifts[0], axis=0)
        page_grid = jnp.roll(page_grid, -shifts[1], axis=1)
        rolled = page_grid.reshape(ROWS, EMB)
        memory = window_block(rolled, 0, shifts[0], shifts[1], norm_gain, qkv_weight, out_weight)
        picked = jnp.take(memory, row_perm, axis=0)
        key_out = jnp.dot(picked, key_weight, preferred_element_type=jnp.float32).astype(jnp.bfloat16)
        value_out = jnp.dot(picked, value_weight, preferred_element_type=jnp.float32).astype(jnp.bfloat16)
        return (key_out, value_out)
    key_rows, value_rows = lax.map(per_page, (memory_in, shift_offsets, row_order))
    return (key_rows, value_rows)
```

```python
import functools

import jax
import jax.numpy as jnp
from jax import lax
from jax.experimental import pallas as pl
from jax.experimental.pallas import tpu as pltpu
from jax.sharding import PartitionSpec as P

HEADS = 16
HEAD_DIM = 32
GRID_H = 28
GRID_W = 21
WIN = 7
ATTN = HEADS * HEAD_DIM
SLOTS = 160
HALO = 64
TOP = 84
GAP = 12
MESH = pl.DeviceIdType.MESH
FAR_FIRST = (2, 1, 3)


def over_21(n):
    return (n * 3121) >> 16


def over_7(n):
    return (n * 9363) >> 16


def group_ids(slot, band, a, c):
    q = jnp.where(slot >= TOP + GAP, slot - GAP, slot)
    valid = (slot < TOP) | ((slot >= TOP + GAP) & (slot < SLOTS - 1))
    row = over_21(q)
    col = q - GRID_W * row
    across = jnp.where(col < c, col - c + GRID_W, col - c)
    wrap_row = jnp.where((row < a) & (band == 3), 2, 0)
    wrap_col = jnp.where(col < c, 1, 0)
    return jnp.where(valid, over_7(across) * 4 + wrap_row + wrap_col, -1)


def kernel(
    n_seq,
    n_tensor,
    shift_ref,
    x_ref,
    gain_ref,
    order_ref,
    qkv_hbm,
    out_hbm,
    key_hbm,
    value_hbm,
    k_out,
    v_out,
    xs,
    top_in,
    low_in,
    normed,
    wq,
    wo,
    wk,
    wv,
    qkv,
    bias,
    att,
    mem,
    k_send,
    v_send,
    k_all,
    v_all,
    chosen,
    k_turn,
    v_turn,
    load_sem,
    halo_send,
    halo_recv,
    seq_send,
    seq_recv,
    turn_send,
    turn_recv,
):
    s = lax.axis_index("seq")
    t = lax.axis_index("tensor")
    cols = k_out.shape[2]
    pos = k_out.shape[1]

    loads = [
        pltpu.make_async_copy(qkv_hbm, wq, load_sem.at[0]),
        pltpu.make_async_copy(out_hbm, wo, load_sem.at[1]),
    ]
    for r in range(n_seq):
        at = pl.ds(pl.multiple_of(lax.rem(s + r, n_seq) * cols, 128), cols)
        loads.append(pltpu.make_async_copy(key_hbm.at[:, at], wk.at[r], load_sem.at[2 + r]))
        loads.append(
            pltpu.make_async_copy(value_hbm.at[:, at], wv.at[r], load_sem.at[2 + n_seq + r])
        )
    for load in loads:
        load.start()

    barrier = pltpu.get_barrier_semaphore()
    for r in range(1, n_seq):
        pl.semaphore_signal(
            barrier, inc=1, device_id={"seq": lax.rem(s + r, n_seq)}, device_id_type=MESH
        )
    for r in range(1, n_tensor):
        pl.semaphore_signal(
            barrier, inc=1, device_id={"tensor": lax.rem(t + r, n_tensor)}, device_id_type=MESH
        )

    a = shift_ref[0, 0]
    c = shift_ref[0, 1]
    late = jnp.where(a >= 4, 1, 0)

    xs[TOP : TOP + GAP] = jnp.zeros((GAP, xs.shape[1]), xs.dtype)
    xs[pl.ds(SLOTS - 16, 16)] = jnp.zeros((16, xs.shape[1]), xs.dtype)
    xs[0:TOP] = x_ref[0:TOP]
    xs[TOP + GAP : SLOTS - 1] = x_ref[TOP : TOP + 63]

    pl.semaphore_wait(barrier, n_seq - 1 + n_tensor - 1)
    up = pltpu.make_async_remote_copy(
        src_ref=xs.at[0:HALO],
        dst_ref=top_in,
        send_sem=halo_send.at[0],
        recv_sem=halo_recv.at[0],
        device_id={"seq": lax.rem(s + n_seq - 1, n_seq)},
        device_id_type=MESH,
    )
    down = pltpu.make_async_remote_copy(
        src_ref=xs.at[SLOTS - HALO : SLOTS],
        dst_ref=low_in,
        send_sem=halo_send.at[1],
        recv_sem=halo_recv.at[1],
        device_id={"seq": lax.rem(s + 1, n_seq)},
        device_id_type=MESH,
    )
    up.start()
    down.start()

    band = lax.rem(s + n_seq - late, n_seq)
    ids_q = group_ids(lax.broadcasted_iota(jnp.int32, (SLOTS, SLOTS), 0), band, a, c)
    ids_k = group_ids(lax.broadcasted_iota(jnp.int32, (SLOTS, SLOTS), 1), band, a, c)
    bias[...] = jnp.where(ids_q == ids_k, 0.0, -1e9)

    order = order_ref[pl.ds(t, 1), :]
    r_row = over_21(order)
    r_col = order - GRID_W * r_row
    r_band = over_7(r_row)
    row = r_row - WIN * r_band + a
    row = jnp.where(row >= WIN, row - WIN, row)
    col = r_col + c
    col = jnp.where(col >= GRID_W, col - GRID_W, col)
    q = row * GRID_W + col
    slot = jnp.where(q >= TOP, q + GAP, q)
    source = (r_band + late) & (n_seq - 1)
    index = source * SLOTS + slot
    for i in range(n_tensor):
        part = index[:, i * pos : (i + 1) * pos]
        part = jnp.concatenate([part, jnp.full((1, 128 - pos), -1, jnp.int32)], axis=1)
        tall = jnp.transpose(jnp.broadcast_to(part, (8, 128)))[:, 0:1]
        places = lax.broadcasted_iota(jnp.int32, (128, n_seq * SLOTS), 1)
        chosen[i] = jnp.where(tall == places, 1.0, 0.0).astype(jnp.bfloat16)

    up.wait()
    down.wait()

    top_end = jnp.where(a <= 3, GRID_W * a, 0)
    low_start = jnp.where(a >= 4, GRID_W * a, 4096) + GAP
    slots_top = lax.broadcasted_iota(jnp.int32, (HALO, xs.shape[1]), 0)
    xs[0:HALO] = jnp.where(
        slots_top < top_end, top_in[...].astype(jnp.float32), xs[0:HALO].astype(jnp.float32)
    ).astype(jnp.bfloat16)
    xs[SLOTS - HALO : SLOTS] = jnp.where(
        slots_top + (SLOTS - HALO) >= low_start,
        low_in[...].astype(jnp.float32),
        xs[SLOTS - HALO : SLOTS].astype(jnp.float32),
    ).astype(jnp.bfloat16)

    def norm(i, carry):
        at = pl.ds(pl.multiple_of(i * 32, 32), 32)
        block = xs[at].astype(jnp.float32)
        mean = jnp.mean(block, axis=-1, keepdims=True)
        block = block - mean
        var = jnp.mean(block * block, axis=-1, keepdims=True)
        normed[at] = (block * lax.rsqrt(var + 1e-05) * gain_ref[...]).astype(jnp.bfloat16)
        return carry

    lax.fori_loop(0, SLOTS // 32, norm, 0)

    loads[0].wait()

    def project(i, carry):
        at = pl.ds(pl.multiple_of(i * 512, 512), 512)
        qkv[:, at] = jnp.dot(
            normed[...], wq[:, at], preferred_element_type=jnp.float32
        ).astype(jnp.bfloat16)
        return carry

    lax.fori_loop(0, 3, project, 0)

    lane_head = lax.broadcasted_iota(jnp.int32, (SLOTS, 128), 1) >> 5

    def attend(g, carry):
        start = pl.multiple_of(g * 128, 128)
        queries = qkv[:, pl.ds(start, 128)]
        keys = qkv[:, pl.ds(start + ATTN, 128)]
        values = qkv[:, pl.ds(start + 2 * ATTN, 128)]
        total = jnp.zeros((SLOTS, 128), jnp.float32)
        for h in range(4):
            own = jnp.where(lane_head == h, 1.0, 0.0).astype(jnp.bfloat16)
            scores = lax.dot_general(
                queries * own, keys, (((1,), (1,)), ((), ())), preferred_element_type=jnp.float32
            )
            scores = scores * HEAD_DIM ** (-0.5) + bias[...]
            top = jnp.max(scores, axis=-1, keepdims=True)
            weights = jnp.exp(scores - top)
            weights = weights / jnp.sum(weights, axis=-1, keepdims=True)
            got = jnp.dot(
                weights.astype(jnp.bfloat16), values, preferred_element_type=jnp.float32
            )
            total = jnp.where(lane_head == h, got, total)
        att[:, pl.ds(start, 128)] = total.astype(jnp.bfloat16)
        return carry

    lax.fori_loop(0, HEADS // 4, attend, 0)

    loads[1].wait()

    def outward(i, carry):
        at = pl.ds(pl.multiple_of(i * 512, 512), 512)
        mem[:, at] = (
            xs[:, at].astype(jnp.float32)
            + jnp.dot(att[...], wo[:, at], preferred_element_type=jnp.float32)
        ).astype(jnp.bfloat16)
        return carry

    lax.fori_loop(0, 2, outward, 0)

    def seq_copy(r, half, slot):
        sent, held = ((k_send, k_all), (v_send, v_all))[half]
        return pltpu.make_async_remote_copy(
            src_ref=sent.at[r - 1],
            dst_ref=held.at[slot],
            send_sem=seq_send.at[half, r - 1],
            recv_sem=seq_recv.at[half, r - 1],
            device_id={"seq": lax.rem(s + r, n_seq)},
            device_id_type=MESH,
        )

    for half, (weight, sent, held) in enumerate(((wk, k_send, k_all), (wv, v_send, v_all))):
        for r in FAR_FIRST:
            loads[2 + 2 * r + half].wait()
            sent[r - 1] = jnp.dot(
                mem[...], weight[r], preferred_element_type=jnp.float32
            ).astype(jnp.bfloat16)
            seq_copy(r, half, s).start()
        loads[2 + half].wait()
        held[s] = jnp.dot(mem[...], weight[0], preferred_element_type=jnp.float32).astype(
            jnp.bfloat16
        )

    def turn_copy(r, half, page):
        sent, held = ((k_turn, k_out), (v_turn, v_out))[half]
        return pltpu.make_async_remote_copy(
            src_ref=sent.at[r - 1],
            dst_ref=held.at[page],
            send_sem=turn_send.at[half, r - 1],
            recv_sem=turn_recv.at[half, r - 1],
            device_id={"tensor": lax.rem(t + r, n_tensor)},
            device_id_type=MESH,
        )

    for half, (held, sent, result) in enumerate(((k_all, k_turn, k_out), (v_all, v_turn, v_out))):
        for r in range(1, n_seq):
            seq_copy(r, half, lax.rem(s + n_seq - r, n_seq)).wait_recv()
        for r in range(1, n_tensor + 1):
            rows = jnp.dot(
                chosen[lax.rem(t + r, n_tensor)],
                held[...].reshape(n_seq * SLOTS, cols),
                preferred_element_type=jnp.float32,
            )[0:pos].astype(jnp.bfloat16)
            if r < n_tensor:
                sent[r - 1] = rows
                turn_copy(r, half, t).start()
            else:
                result[t] = rows

    for half in range(2):
        for r in range(1, n_seq):
            seq_copy(r, half, s).wait_send()
        for r in range(1, n_tensor):
            turn_copy(r, half, lax.rem(t + n_tensor - r, n_tensor)).wait()


def local(
    memory_in, norm_gain, qkv_weight, out_weight, key_weight, value_weight, shift_offsets, row_order
):
    n_seq = lax.axis_size("seq")
    n_tensor = lax.axis_size("tensor")
    width = memory_in.shape[2]
    cols = key_weight.shape[1] // n_seq
    pos = row_order.shape[1] // n_tensor
    bf16 = jnp.bfloat16
    vmem = pl.BlockSpec(memory_space=pltpu.VMEM)
    away = pl.BlockSpec(memory_space=pl.ANY)
    out = jax.ShapeDtypeStruct((n_tensor, pos, cols), bf16)
    return pl.pallas_call(
        functools.partial(kernel, n_seq, n_tensor),
        out_shape=(out, out),
        in_specs=[
            pl.BlockSpec(memory_space=pltpu.SMEM),
            vmem,
            vmem,
            vmem,
            away,
            away,
            away,
            away,
        ],
        out_specs=(vmem, vmem),
        scratch_shapes=[
            pltpu.VMEM((SLOTS, width), bf16),
            pltpu.VMEM((HALO, width), bf16),
            pltpu.VMEM((HALO, width), bf16),
            pltpu.VMEM((SLOTS, width), bf16),
            pltpu.VMEM((width, 3 * ATTN), bf16),
            pltpu.VMEM((ATTN, width), bf16),
            pltpu.VMEM((n_seq, width, cols), bf16),
            pltpu.VMEM((n_seq, width, cols), bf16),
            pltpu.VMEM((SLOTS, 3 * ATTN), bf16),
            pltpu.VMEM((SLOTS, SLOTS), jnp.float32),
            pltpu.VMEM((SLOTS, ATTN), bf16),
            pltpu.VMEM((SLOTS, width), bf16),
            pltpu.VMEM((n_seq - 1, SLOTS, cols), bf16),
            pltpu.VMEM((n_seq - 1, SLOTS, cols), bf16),
            pltpu.VMEM((n_seq, SLOTS, cols), bf16),
            pltpu.VMEM((n_seq, SLOTS, cols), bf16),
            pltpu.VMEM((n_tensor, 128, n_seq * SLOTS), bf16),
            pltpu.VMEM((n_tensor - 1, pos, cols), bf16),
            pltpu.VMEM((n_tensor - 1, pos, cols), bf16),
            pltpu.SemaphoreType.DMA((2 + 2 * n_seq,)),
            pltpu.SemaphoreType.DMA((2,)),
            pltpu.SemaphoreType.DMA((2,)),
            pltpu.SemaphoreType.DMA((2, n_seq - 1)),
            pltpu.SemaphoreType.DMA((2, n_seq - 1)),
            pltpu.SemaphoreType.DMA((2, n_tensor - 1)),
            pltpu.SemaphoreType.DMA((2, n_tensor - 1)),
        ],
        compiler_params=pltpu.CompilerParams(
            collective_id=0, has_side_effects=True, vmem_limit_bytes=60 * 1024 * 1024
        ),
        name="encode_to_kv",
    )(
        shift_offsets,
        memory_in.reshape(memory_in.shape[1:]),
        norm_gain.reshape(1, width),
        row_order,
        qkv_weight,
        out_weight,
        key_weight,
        value_weight,
    )


def solution(mesh):
    placed = (
        P(("dp", "tensor"), "seq", None),
        P(),
        P(),
        P(),
        P(),
        P(),
        P(("dp", "tensor"), None),
        P("dp", None),
    )
    return jax.shard_map(
        local,
        mesh=mesh,
        in_specs=placed,
        out_specs=(P("dp", "tensor", "seq"), P("dp", "tensor", "seq")),
        check_vma=False,
    )
```
